32 devices in a mesh: dp: 4 (over y, x), vocab: 8 (over z, core).
Axes of the slice: x: 2, y: 2, z: 4, core: 2. Of those that a mesh axis runs over, the one named last changes fastest.
Arguments:
- cotangent: bfloat16 [16384, 4608], P(('dp', 'vocab')), may hold values from -6 to 6
- token_owner: int32 [16384, 1], P(('dp', 'vocab')), may hold values from 0 to 7; in each aligned block of 512 rows (0 to 511, 512 to 1023, ...) at most 128 rows name the same one
- token_row: int32 [16384], P(('dp', 'vocab')), may hold values from 0 to 511
- params: float32 [4096, 4608], P('vocab', 'dp'), may hold values from -6 to 6
- moment_one: float32 [4096, 4608], P('vocab', 'dp'), may hold values from -4 to 4
- moment_two: float32 [4096, 4608], P('vocab', 'dp'), may hold values from 0.01 to 1
Outputs:
- new_params: float32 [4096, 4608], P('vocab', 'dp')
- new_first: float32 [4096, 4608], P('vocab', 'dp')
- new_second: float32 [4096, 4608], P('vocab', 'dp')
The draws below stay inside these ranges and needn't reach their ends.
Inputs may be any that keep to these rules, and one draw needn't show every extreme that they name: `token_owner`: among the tokens of one device, no owner is named more than 128 times, a bound that some block reaches.
All inputs are finite; a program needn't handle non-finite values.
Results may differ from the reference program's by a relative error of at most 0.0003.
Values may be sent and summed in bfloat16 or wider, within the bound.
A program may use at most 192 MiB of HBM per device.

```python
import math
import jax
import jax.numpy as jnp
import numpy as np

D = 4608
TOK_DEV = 512
OWN_ROWS = 512
CAP = 128
TOKENS = 16384
ROWS = 4096
N_VOCAB = 8


def set_ends(entries, stream_key, low, high):
    shape = entries.shape
    spot = [jax.random.randint(jax.random.fold_in(stream_key, axis), (), 0, shape[axis]) for axis in range(len(shape))]
    entries = entries.at[tuple(spot)].set(low)
    longest = shape.index(max(shape))
    spot[longest] = (spot[longest] + 1) % shape[longest]
    return entries.at[tuple(spot)].set(high)


def shard_levels(rng, extent, pieces, low, high):
    def one(axis_at, blocks):
        heights = jax.random.uniform(jax.random.fold_in(jax.random.fold_in(rng, 6), axis_at), (blocks,), jnp.float32, low / len(pieces), high / len(pieces))
        return jnp.repeat(jnp.exp(heights), extent[axis_at] // blocks).reshape((-1,) + (1,) * (len(extent) - axis_at - 1))

    level = one(*pieces[0])
    for cut in pieces[1:]:
        level = level * one(*cut)
    return level


def assign_block(own_key, own, number, rows, number_of, top, most, lean):
    sequence = jax.random.permutation(own_key, number_of)
    crowded, ordinary = portions_of(number_of, rows * top, most, lean, True), portions_of(number_of, rows * top, most, lean, False)
    places = jnp.arange(number_of)

    def named(lengths, rotation):
        used = int((lengths > 0).sum())
        fixed = max(1, used // 4)
        shifted = fixed + (places - fixed + rotation * (used - fixed)) % max(1, number_of - fixed)
        return jnp.zeros((number_of,), jnp.int32).at[sequence[jnp.where(places < fixed, places, shifted)]].set(jnp.asarray(lengths, jnp.int32))

    lengths = jnp.where(number % 4 == 0, named(crowded, number // 4), named(ordinary, number - number // 4 - 1))
    mixed = jax.random.permutation(jax.random.fold_in(own, 3), number_of)
    giver, taker = mixed[0:number_of // 2 * 2:2], mixed[1:number_of // 2 * 2:2]
    margin = jnp.minimum(lengths[giver] - 1, most - lengths[taker]) // 2
    margin = jnp.where((giver == sequence[0]) | (taker == sequence[0]) | (lengths[taker] == 0), 0, jnp.maximum(margin, 0))
    shifted = jax.random.randint(jax.random.fold_in(own, 4), (number_of // 2,), 0, 1 << 20) % (margin + 1)
    lengths = lengths.at[giver].add(-shifted).at[taker].add(shifted)
    labels = jnp.searchsorted(jnp.cumsum(lengths), jnp.arange(rows * top), side="right").astype(jnp.int32)
    grid = labels.reshape(top, rows).T
    grid = grid[jax.random.permutation(jax.random.fold_in(own, 1), rows)]
    rotation = jax.random.randint(jax.random.fold_in(own, 2), (rows, 1), 0, top)
    return jnp.take_along_axis(grid, (jnp.arange(top)[None, :] + rotation) % top, axis=1)


def portions_of(amount, total, bound, slope, full):
    weights = [(1 << 20) // math.isqrt(grade ** slope) + 1 for grade in range(1, amount + 1)]
    largest = bound if full else min(bound, max(-(-total // amount), total * weights[0] // sum(weights)))
    least = 1 if total - largest >= amount - 1 else 0
    counts, rest = [largest] + [least] * (amount - 1), total - largest - least * (amount - 1)
    while rest > 0:
        candidates = [i for i in range(1, amount) if counts[i] < largest] or [i for i in range(1, amount) if counts[i] < bound]
        whole, remaining = sum([weights[i] for i in candidates]), rest
        for i in candidates:
            addition = min(bound - counts[i], max(1, remaining * weights[i] // whole), rest)
            counts[i] = counts[i] + addition
            rest = rest - addition
    return np.array(counts)


def gaussian(stream_key, shape, scale, reach, shards=(), kind=jnp.bfloat16):
    gain = shard_levels(stream_key, shape, shards, -0.22, 0.18) if shards else 1.0
    drawn = jax.random.normal(stream_key, shape, jnp.float32) * scale * gain
    return jnp.minimum(jnp.maximum(drawn, -reach), reach).astype(kind)


def setup_inputs(seed: int = 0) -> dict:
    arg_keys = jax.random.split(jax.random.key(seed), 7)
    cotangent = gaussian(arg_keys[0], (TOKENS, D), 1.0, 6.0, ((0, 32),))
    token_owner_keys = jax.random.split(jax.random.fold_in(arg_keys[1], 1), TOKENS // TOK_DEV)
    token_owner_turns = jax.random.permutation(jax.random.fold_in(arg_keys[1], 3), TOKENS // TOK_DEV)
    token_owner = jax.vmap(lambda own, number: assign_block(jax.random.fold_in(arg_keys[1], 2), own, number, TOK_DEV, N_VOCAB, 1, CAP, 1))(token_owner_keys, token_owner_turns).reshape((TOKENS, 1))
    token_row = set_ends(jax.random.randint(arg_keys[2], (TOKENS,), 0, OWN_ROWS), jax.random.fold_in(arg_keys[2], 1), 0, OWN_ROWS - 1).astype(jnp.int32)
    params = gaussian(arg_keys[3], (ROWS, D), 1.0, 6.0, ((0, 8), (1, 4)), jnp.float32)
    moment_one = gaussian(arg_keys[4], (ROWS, D), 0.3, 4.0, ((0, 8), (1, 4)), jnp.float32)
    moment_two = jnp.clip(jnp.exp(math.log(1.0) - 4.6051702 * jax.random.uniform(arg_keys[5], (ROWS, D), jnp.float32) ** shard_levels(arg_keys[5], (ROWS, D), ((0, 8), (1, 4)), -0.2, 0.2)), 0.01, 1.0)
    return {"cotangent": cotangent, "token_owner": token_owner, "token_row": token_row, "params": params, "moment_one": moment_one, "moment_two": moment_two}


beta_first = 0.9
beta_second = 0.999
learning = 0.01
epsilon = 1e-08
correct_second = 0.6323045752290363

def reference(cotangent, token_owner, token_row, params, moment_one, moment_two):
    target = (token_owner[:, 0] * OWN_ROWS + token_row).astype(jnp.int32)
    grads = jax.ops.segment_sum(cotangent.astype(jnp.float32), target, num_segments=ROWS)
    new_first = beta_first * moment_one + (1.0 - beta_first) * grads
    new_second = beta_second * moment_two + (1.0 - beta_second) * grads * grads
    step_size = new_first / (jnp.sqrt(new_second / correct_second) + epsilon)
    new_params = params - learning * step_size
    return (new_params, new_first, new_second)
```

```python
import functools

import jax
import jax.numpy as jnp
from jax import lax
from jax.experimental import pallas as pl
from jax.experimental.pallas import tpu as pltpu
from jax.sharding import PartitionSpec as P

beta_first = 0.9
beta_second = 0.999
learning = 0.01
epsilon = 1e-08
correct_second = 0.6323045752290363

LANES = 128
TILE = 128
VMEM_MIB = 46
SHARES = (0, 1, 2, 4, 6, 9)
MESH = pl.DeviceIdType.MESH


def bucket(cotangent, owner_list, token_row, owners, capacity):
    owner_hot = (owner_list[:, None] == jnp.arange(owners, dtype=jnp.int32)[None, :]).astype(
        jnp.int32
    )
    order = jnp.arange(owner_list.shape[0], dtype=jnp.int32)
    before = (order[None, :] < order[:, None]).astype(jnp.bfloat16)
    earlier = jnp.dot(
        before, owner_hot.astype(jnp.bfloat16), preferred_element_type=jnp.float32
    ).astype(jnp.int32)
    slot_index = jnp.sum(earlier * owner_hot, axis=1)
    target = owner_list * capacity + slot_index
    places = jnp.arange(owners * capacity, dtype=jnp.int32)
    matches = places[:, None] == target[None, :]
    outgoing = jnp.dot(matches.astype(jnp.bfloat16), cotangent, preferred_element_type=jnp.float32)
    outgoing = outgoing.astype(jnp.bfloat16).reshape(owners, capacity, cotangent.shape[1])
    row_index = jnp.max(jnp.where(matches, token_row[None, :], -1), axis=1).reshape(
        owners, capacity
    )
    return (outgoing, row_index)


def adam(grads, params, moment_one, moment_two):
    new_first = beta_first * moment_one + (1.0 - beta_first) * grads
    new_second = beta_second * moment_two + (1.0 - beta_second) * grads * grads
    step_size = new_first / (jnp.sqrt(new_second / correct_second) + epsilon)
    new_params = params - learning * step_size
    return (new_params, new_first, new_second)


def local_general(cotangent, token_owner, token_row, params, moment_one, moment_two):
    owners = lax.axis_size("vocab")
    tok_count, width = cotangent.shape
    capacity = 2 * tok_count // owners
    own_rows = params.shape[0]
    outgoing, row_index = bucket(cotangent, token_owner[:, 0], token_row, owners, capacity)
    arrived, arrived_rows = (
        lax.all_to_all(outgoing, "vocab", split_axis=0, concat_axis=0, tiled=True),
        lax.all_to_all(row_index, "vocab", split_axis=0, concat_axis=0, tiled=True),
    )
    selector = (
        jnp.arange(own_rows, dtype=jnp.int32)[:, None] == arrived_rows.reshape(-1)[None, :]
    ).astype(jnp.bfloat16)
    full_grads = jnp.dot(
        selector, arrived.reshape(owners * capacity, width), preferred_element_type=jnp.float32
    )
    grads = lax.psum_scatter(full_grads, "dp", scatter_dimension=1, tiled=True)
    return adam(grads, params, moment_one, moment_two)


def flipped(index, bits):
    bit = 1
    while bit <= bits:
        if bits & bit:
            index = index + bit * (1 - 2 * lax.rem(lax.div(index, bit), 2))
        bit *= 2
    return index


def line_kernel(
    slices, chunks, tile, owner_ref, row_ref, cot_ref, out_ref,
    held, owner_of, row_of, sel, acc, tx, txs, rx, rxs,
    xy_send, xy_recv, code_send, code_recv, relay_send, relay_recv, own_sem,
    z_send, z_recv, s_send, s_recv,
):
    d = lax.axis_index("dp")
    v = lax.axis_index("vocab")
    z, core = lax.div(v, 2), lax.rem(v, 2)
    partner = flipped(v, 1)
    toks = cot_ref.shape[0]
    own_rows, cols = out_ref.shape
    half = slices * toks
    edge = (z == 0) | (z == 3)
    inner = (z == 1) | (z == 2)
    low = lax.div(z, 2)
    mid_z, far_z = 2 - low, 3 - 3 * low
    near_z = flipped(z, 1)

    def at(dp, vocab):
        return {"dp": dp, "vocab": vocab}

    barrier = pltpu.get_barrier_semaphore()
    greeted = [at(flipped(d, s), flipped(v, k)) for s in range(slices) for k in range(2) if s or k]
    greeted += [at(d, lax.rem(v + 2 * s, 8)) for s in range(1, 4)]
    for peer in greeted:
        pl.semaphore_signal(barrier, inc=1, device_id=peer, device_id_type=MESH)
    pl.semaphore_wait(barrier, len(greeted))

    def remote(src, dst, send, recv, peer):
        return pltpu.make_async_remote_copy(
            src_ref=src, dst_ref=dst, send_sem=send, recv_sem=recv, device_id=peer,
            device_id_type=MESH,
        )

    def code_copies(b):
        k, s = b // slices, b % slices
        pairs = ((owner_ref, owner_of), (row_ref, row_of))
        if b == 0:
            return [
                pltpu.make_async_copy(src, dst.at[0], code_recv.at[n, 0])
                for n, (src, dst) in enumerate(pairs)
            ]
        peer = at(flipped(d, s), flipped(v, k))
        return [
            remote(src, dst.at[b], code_send.at[n, b], code_recv.at[n, b], peer)
            for n, (src, dst) in enumerate(pairs)
        ]

    def xy_copy(c, s):
        start, size = chunks[c]
        if s == 0:
            first = pl.multiple_of(d * cols + start, LANES)
            return pltpu.make_async_copy(
                cot_ref.at[:, pl.ds(first, size)],
                held.at[pl.ds(0, toks), pl.ds(start, size)], own_sem.at[c],
            )
        peer = flipped(d, s)
        first = pl.multiple_of(peer * cols + start, LANES)
        return remote(
            cot_ref.at[:, pl.ds(first, size)], held.at[pl.ds(s * toks, toks), pl.ds(start, size)],
            xy_send.at[c, s], xy_recv.at[c, s], at(peer, v),
        )

    def relay_copy(c):
        start, size = chunks[c]
        return remote(
            held.at[pl.ds(0, half), pl.ds(start, size)],
            held.at[pl.ds(half, half), pl.ds(start, size)],
            relay_send.at[c], relay_recv.at[c], at(d, partner),
        )

    def line_copies(c, i, slot, to):
        start, size = chunks[c]
        lanes = pl.ds(start, size)
        peer = at(d, to * 2 + core)
        return (
            remote(tx.at[i, :, lanes], rx.at[slot, :, lanes], z_send.at[c, i], z_recv.at[c, slot], peer),
            remote(txs.at[i, :, lanes], rxs.at[slot, :, lanes], s_send.at[c, i], s_recv.at[c, slot], peer),
        )

    def send_line(c, i, slot, to):
        for copy in line_copies(c, i, slot, to):
            copy.start()

    def await_line(c, slot):
        for copy in line_copies(c, 0, slot, near_z):
            copy.wait_recv()

    def quantize(c, i, top):
        start, size = chunks[c]
        lanes = pl.ds(start, size)
        wide = pl.ds(0, size)
        bound = jnp.maximum(top, 1e-30)
        txs[i, :, lanes] = jnp.broadcast_to(bound * (1.0 / 32767.0), (8, size))
        factor = 32767.0 / bound

        @pl.loop(0, own_rows // tile)
        def _(r):
            rows = pl.ds(pl.multiple_of(r * tile, tile), tile)
            scaled = jnp.round(acc[i, rows, wide] * factor)
            tx[i, rows, lanes] = scaled.astype(jnp.int32).astype(jnp.int16)

    def partial(c, i):
        start, size = chunks[c]
        lanes = pl.ds(start, size)

        def body(r, top):
            rows = pl.ds(pl.multiple_of(r * tile, tile), tile)
            part = jnp.dot(sel[i, rows, :], held[:, lanes], preferred_element_type=jnp.float32)
            if i == 3:
                out_ref[rows, lanes] = part
            else:
                acc[i, rows, pl.ds(0, size)] = part
            return jnp.maximum(top, jnp.max(jnp.abs(part), axis=0, keepdims=True))

        return lax.fori_loop(0, own_rows // tile, body, jnp.zeros((1, size), jnp.float32))

    for b in range(2 * slices):
        for copy in code_copies(b):
            copy.start()
    for c in range(len(chunks)):
        for s in [*range(1, slices), 0]:
            xy_copy(c, s).start()

    places = (near_z, mid_z, far_z, z)

    def build(i):
        base = (places[i] * 2 + core) * own_rows
        for b in range(2 * slices):
            code = owner_of[b] * own_rows + row_of[b] - base

            @pl.loop(0, own_rows // tile)
            def _(r):
                first = pl.multiple_of(r * tile, tile)
                rows = lax.broadcasted_iota(jnp.int32, (tile, toks), 0)
                sel[i, pl.ds(first, tile), pl.ds(b * toks, toks)] = jnp.where(
                    rows == code - first, 1.0, 0.0
                ).astype(jnp.bfloat16)

    def start_relay(c):
        for s in range(slices):
            if s:
                xy_copy(c, s).wait_recv()
            else:
                xy_copy(c, s).wait()
        relay_copy(c).start()

    def add(c, slots):
        start, size = chunks[c]
        lanes = pl.ds(start, size)
        for slot in slots:
            await_line(c, slot)
        scales = [rxs[slot, 0:1, lanes] for slot in slots]

        @pl.loop(0, own_rows // tile)
        def _(r):
            rows = pl.ds(pl.multiple_of(r * tile, tile), tile)
            total = out_ref[rows, lanes]
            for slot, scale in zip(slots, scales):
                total = total + rx[slot, rows, lanes].astype(jnp.float32) * scale
            out_ref[rows, lanes] = total

    for b in range(2 * slices):
        for copy in code_copies(b):
            if b:
                copy.wait_recv()
            else:
                copy.wait()
    build(2)
    build(1)
    start_relay(0)
    build(0)
    for c in range(len(chunks)):
        start, size = chunks[c]
        lanes = pl.ds(start, size)
        relay_copy(c).wait_recv()
        top = partial(c, 2)

        @pl.when(edge)
        def _():
            quantize(c, 2, top)
            send_line(c, 2, 1, near_z)

        quantize(c, 1, partial(c, 1))
        pl.when(edge)(lambda: send_line(c, 1, 2, mid_z))
        pl.when(inner)(lambda: send_line(c, 1, 3, mid_z))
        quantize(c, 0, partial(c, 0))
        send_line(c, 0, 0, near_z)
        if c == 0:
            build(3)
        partial(c, 3)
        if c + 1 < len(chunks):
            start_relay(c + 1)

        @pl.when(inner)
        def _():
            if c >= 2:
                add(c - 2, (3, 2, 0))
            await_line(c, 1)
            scale = rxs[1, 0:1, lanes]

            def body(r, top):
                rows = pl.ds(pl.multiple_of(r * tile, tile), tile)
                both = acc[2, rows, pl.ds(0, size)] + rx[1, rows, lanes].astype(jnp.float32) * scale
                acc[2, rows, pl.ds(0, size)] = both
                return jnp.maximum(top, jnp.max(jnp.abs(both), axis=0, keepdims=True))

            top = lax.fori_loop(0, own_rows // tile, body, jnp.zeros((1, size), jnp.float32))
            quantize(c, 2, top)
            send_line(c, 2, 1, far_z)

    last = len(chunks)

    @pl.when(inner)
    def _():
        for c in range(max(last - 2, 0), last):
            add(c, (3, 2, 0))

    @pl.when(edge)
    def _():
        for c in range(last):
            add(c, (0, 1))

    for b in range(1, 2 * slices):
        for copy in code_copies(b):
            copy.wait_send()
    for c in range(len(chunks)):
        for s in range(1, slices):
            xy_copy(c, s).wait_send()
        relay_copy(c).wait_send()
        for i in range(3):
            for copy in line_copies(c, i, 0, near_z):
                copy.wait_send()


def local_line(cotangent, token_owner, token_row, params, moment_one, moment_two):
    slices = lax.axis_size("dp")
    toks = cotangent.shape[0]
    own_rows, cols = params.shape
    tiles = cols // LANES
    marks = sorted({tiles * share // SHARES[-1] for share in SHARES})
    chunks = [(a * LANES, (b - a) * LANES) for a, b in zip(marks[:-1], marks[1:])]
    count = len(chunks)
    dma = pltpu.SemaphoreType.DMA
    operands = (token_owner.reshape(1, toks), token_row.reshape(1, toks), cotangent)
    grads = pl.pallas_call(
        functools.partial(line_kernel, slices, chunks, TILE),
        out_shape=jax.ShapeDtypeStruct((own_rows, cols), jnp.float32),
        in_specs=[pl.BlockSpec(memory_space=pltpu.HBM)] * 3,
        out_specs=pl.BlockSpec(memory_space=pltpu.VMEM),
        scratch_shapes=[
            pltpu.VMEM((2 * slices * toks, cols), jnp.bfloat16),
            pltpu.VMEM((2 * slices, 1, toks), jnp.int32),
            pltpu.VMEM((2 * slices, 1, toks), jnp.int32),
            pltpu.VMEM((4, own_rows, 2 * slices * toks), jnp.bfloat16),
            pltpu.VMEM((3, own_rows, max(size for _, size in chunks)), jnp.float32),
            pltpu.VMEM((3, own_rows, cols), jnp.int16),
            pltpu.VMEM((3, 8, cols), jnp.float32),
            pltpu.VMEM((4, own_rows, cols), jnp.int16),
            pltpu.VMEM((4, 8, cols), jnp.float32),
            dma((count, slices)), dma((count, slices)),
            dma((2, 2 * slices)), dma((2, 2 * slices)),
            dma((count,)), dma((count,)), dma((count,)),
            dma((count, 3)), dma((count, 4)), dma((count, 3)), dma((count, 4)),
        ],
        name="line_sums",
        compiler_params=pltpu.CompilerParams(
            collective_id=0, has_side_effects=True, vmem_limit_bytes=VMEM_MIB * 1024 * 1024
        ),
    )(*(pltpu.with_memory_space_constraint(a, pltpu.HBM) for a in operands))
    return adam(grads, params, moment_one, moment_two)


def solution(mesh):
    placed = (
        P(("dp", "vocab"), None),
        P(("dp", "vocab"), None),
        P(("dp", "vocab")),
        P("vocab", "dp"),
        P("vocab", "dp"),
        P("vocab", "dp"),
    )
    slices = mesh.shape["dp"]
    line = mesh.shape["vocab"] == 2 * 4 and slices & (slices - 1) == 0
    return jax.shard_map(
        local_line if line else local_general,
        mesh=mesh,
        in_specs=placed,
        out_specs=(P("vocab", "dp"), P("vocab", "dp"), P("vocab", "dp")),
        check_vma=False,
    )
```

```python
import functools

import jax
import jax.numpy as jnp
from jax import lax
from jax.experimental import pallas as pl
from jax.experimental.pallas import tpu as pltpu
from jax.sharding import PartitionSpec as P

beta_first = 0.9
beta_second = 0.999
learning = 0.01
epsilon = 1e-08
correct_second = 0.6323045752290363

LANES = 128
TILE = 128
DOT_TILE = 256
LEVELS = 32767.0
VMEM_MIB = 46
SHARES = (0, 1, 2, 3, 5, 7, 8, 9)
MESH = pl.DeviceIdType.MESH


def bucket(cotangent, owner_list, token_row, owners, capacity):
    owner_hot = (owner_list[:, None] == jnp.arange(owners, dtype=jnp.int32)[None, :]).astype(
        jnp.int32
    )
    order = jnp.arange(owner_list.shape[0], dtype=jnp.int32)
    before = (order[None, :] < order[:, None]).astype(jnp.bfloat16)
    earlier = jnp.dot(
        before, owner_hot.astype(jnp.bfloat16), preferred_element_type=jnp.float32
    ).astype(jnp.int32)
    slot_index = jnp.sum(earlier * owner_hot, axis=1)
    target = owner_list * capacity + slot_index
    places = jnp.arange(owners * capacity, dtype=jnp.int32)
    matches = places[:, None] == target[None, :]
    outgoing = jnp.dot(matches.astype(jnp.bfloat16), cotangent, preferred_element_type=jnp.float32)
    outgoing = outgoing.astype(jnp.bfloat16).reshape(owners, capacity, cotangent.shape[1])
    row_index = jnp.max(jnp.where(matches, token_row[None, :], -1), axis=1).reshape(
        owners, capacity
    )
    return (outgoing, row_index)


def adam(grads, params, moment_one, moment_two):
    new_first = beta_first * moment_one + (1.0 - beta_first) * grads
    new_second = beta_second * moment_two + (1.0 - beta_second) * grads * grads
    step_size = new_first / (jnp.sqrt(new_second / correct_second) + epsilon)
    new_params = params - learning * step_size
    return (new_params, new_first, new_second)


def local_general(cotangent, token_owner, token_row, params, moment_one, moment_two):
    owners = lax.axis_size("vocab")
    tok_count, width = cotangent.shape
    capacity = 2 * tok_count // owners
    own_rows = params.shape[0]
    outgoing, row_index = bucket(cotangent, token_owner[:, 0], token_row, owners, capacity)
    arrived, arrived_rows = (
        lax.all_to_all(outgoing, "vocab", split_axis=0, concat_axis=0, tiled=True),
        lax.all_to_all(row_index, "vocab", split_axis=0, concat_axis=0, tiled=True),
    )
    selector = (
        jnp.arange(own_rows, dtype=jnp.int32)[:, None] == arrived_rows.reshape(-1)[None, :]
    ).astype(jnp.bfloat16)
    full_grads = jnp.dot(
        selector, arrived.reshape(owners * capacity, width), preferred_element_type=jnp.float32
    )
    grads = lax.psum_scatter(full_grads, "dp", scatter_dimension=1, tiled=True)
    return adam(grads, params, moment_one, moment_two)


def flipped(index, bits):
    bit = 1
    while bit <= bits:
        if bits & bit:
            index = index + bit * (1 - 2 * lax.rem(lax.div(index, bit), 2))
        bit *= 2
    return index


def line_kernel(
    slices, chunks, owner_ref, row_ref, cot_ref, out_ref,
    held, owner_own, row_own, code_of, sel, acc, tx, txs, rx, rxs,
    own_sem, code_send, code_recv, xy_send, xy_recv, relay_send, relay_recv, z_send, z_recv, s_send, s_recv,
):
    d = lax.axis_index("dp")
    v = lax.axis_index("vocab")
    z, core = lax.div(v, 2), lax.rem(v, 2)
    partner = flipped(v, 1)
    toks = cot_ref.shape[0]
    own_rows, cols = out_ref.shape
    half = slices * toks
    last = len(chunks) - 1
    edge = (z == 0) | (z == 3)
    inner = (z == 1) | (z == 2)
    low = lax.div(z, 2)
    mid_z, far_z = 2 - low, 3 - 3 * low
    near_z = flipped(z, 1)
    places = (near_z, mid_z, far_z, z)

    def at(dp, vocab):
        return {"dp": dp, "vocab": vocab}

    def remote(src, dst, send, recv, peer):
        return pltpu.make_async_remote_copy(
            src_ref=src, dst_ref=dst, send_sem=send, recv_sem=recv, device_id=peer,
            device_id_type=MESH,
        )

    def span(c):
        start, size = chunks[c]
        return pl.ds(start, size)

    def code_copy(s):
        return remote(
            code_of.at[0], code_of.at[s], code_send.at[s], code_recv.at[s], at(flipped(d, s), v)
        )

    def code_relay():
        return remote(
            code_of.at[pl.ds(0, slices)], code_of.at[pl.ds(slices, slices)],
            code_send.at[0], code_recv.at[0], at(d, partner),
        )

    def xy_copy(c, s):
        start, size = chunks[c]
        peer = flipped(d, s)
        first = pl.multiple_of(peer * cols + start, LANES)
        return remote(
            cot_ref.at[:, pl.ds(first, size)], held.at[pl.ds(s * toks, toks), span(c)],
            xy_send.at[c, s], xy_recv.at[c, s], at(peer, v),
        )

    def relay_copies(c):
        pieces = [(s * toks, toks) for s in [*reversed(range(1, slices)), 0]] if c == 0 else [(0, half)]
        return [
            remote(
                held.at[pl.ds(row, size), span(c)], held.at[pl.ds(half + row, size), span(c)],
                relay_send.at[c, n], relay_recv.at[c, n], at(d, partner),
            )
            for n, (row, size) in enumerate(pieces)
        ]

    def line_copies(c, i, slot, to):
        peer = at(d, to * 2 + core)
        return (
            remote(
                txs.at[i, :, span(c)], rxs.at[slot, :, span(c)],
                s_send.at[c, i], s_recv.at[c, slot], peer,
            ),
            remote(
                tx.at[i, :, span(c)], rx.at[slot, :, span(c)],
                z_send.at[c, i], z_recv.at[c, slot], peer,
            ),
        )

    def start_xy(c):
        for s in reversed(range(1, slices)):
            xy_copy(c, s).start()

    def start_relay(c):
        copies = relay_copies(c)
        if c == 0:
            copies.pop().start()
        for s in reversed(range(1, slices)):
            xy_copy(c, s).wait_recv()
            if c == 0:
                copies.pop(0).start()
        if c:
            copies[0].start()

    first = pl.multiple_of(d * cols, LANES)
    own_copies = [
        pltpu.make_async_copy(owner_ref, owner_own, own_sem.at[0]),
        pltpu.make_async_copy(row_ref, row_own, own_sem.at[1]),
        pltpu.make_async_copy(
            cot_ref.at[:, pl.ds(first, cols)], held.at[pl.ds(0, toks), :], own_sem.at[2]
        ),
    ]
    for copy in own_copies:
        copy.start()

    barrier = pltpu.get_barrier_semaphore()
    greeted = [at(flipped(d, s), v) for s in range(1, slices)] + [at(d, partner)]
    greeted += [at(d, lax.rem(v + 2 * s, 8)) for s in range(1, 4)]
    for peer in greeted:
        pl.semaphore_signal(barrier, inc=1, device_id=peer, device_id_type=MESH)
    own_copies[0].wait()
    own_copies[1].wait()
    code_of[0] = owner_own[...] * own_rows + row_own[...]
    pl.semaphore_wait(barrier, len(greeted))

    for s in reversed(range(1, slices)):
        code_copy(s).start()
    start_xy(0)
    if last >= 1:
        start_xy(1)
    for s in range(1, slices):
        code_copy(s).wait_recv()
    code_relay().start()
    own_copies[2].wait()

    def build(i, parts):
        base = (places[i] * 2 + core) * own_rows
        for b in parts:
            code = code_of[b] - base

            @pl.loop(0, own_rows // TILE)
            def _(r):
                first = pl.multiple_of(r * TILE, TILE)
                rows = lax.broadcasted_iota(jnp.int32, (TILE, toks), 0)
                sel[i, pl.ds(first, TILE), pl.ds(b * toks, toks)] = jnp.where(
                    rows == code - first, 1.0, 0.0
                ).astype(jnp.bfloat16)

    def partial(c, i, tokens=None, base=False):
        start, size = chunks[c]
        tokens = pl.ds(0, 2 * half) if tokens is None else tokens

        def body(r, top):
            rows = pl.ds(pl.multiple_of(r * DOT_TILE, DOT_TILE), DOT_TILE)
            part = jnp.dot(
                sel[i, rows, tokens], held[tokens, span(c)], preferred_element_type=jnp.float32
            )
            if base:
                part = part + acc[c % 2, i, rows, pl.ds(0, size)]
            if i == 3:
                out_ref[rows, span(c)] = part
            else:
                acc[c % 2, i, rows, pl.ds(0, size)] = part
            return jnp.maximum(top, jnp.max(jnp.abs(part), axis=0, keepdims=True))

        return lax.fori_loop(0, own_rows // DOT_TILE, body, jnp.zeros((1, size), jnp.float32))

    def send(c, i, top, slot, to):
        start, size = chunks[c]
        bound = jnp.maximum(top, 1e-30)
        txs[i, :, span(c)] = bound * (1.0 / LEVELS)
        factor = LEVELS / bound

        @pl.loop(0, own_rows // TILE)
        def _(r):
            rows = pl.ds(pl.multiple_of(r * TILE, TILE), TILE)
            scaled = jnp.round(acc[c % 2, i, rows, pl.ds(0, size)] * factor)
            tx[i, rows, span(c)] = scaled.astype(jnp.int32).astype(jnp.int16)

        for copy in line_copies(c, i, slot, to):
            copy.start()

    def arrived(c, slot):
        for copy in line_copies(c, 0, slot, near_z):
            copy.wait_recv()
        return rxs[slot, :, span(c)]

    def combine(c, i, rx_slot, slot, to):
        start, size = chunks[c]
        scale = arrived(c, rx_slot)

        def body(r, top):
            rows = pl.ds(pl.multiple_of(r * TILE, TILE), TILE)
            wide = pl.ds(0, size)
            both = acc[c % 2, i, rows, wide] + rx[rx_slot, rows, span(c)].astype(jnp.float32) * scale
            acc[c % 2, i, rows, wide] = both
            return jnp.maximum(top, jnp.max(jnp.abs(both), axis=0, keepdims=True))

        top = lax.fori_loop(0, own_rows // TILE, body, jnp.zeros((1, size), jnp.float32))
        send(c, i, top, slot, to)

    def add(c, slots):
        scales = [arrived(c, slot) for slot in slots]

        @pl.loop(0, own_rows // TILE)
        def _(r):
            rows = pl.ds(pl.multiple_of(r * TILE, TILE), TILE)
            total = out_ref[rows, span(c)]
            for slot, scale in zip(slots, scales):
                total = total + rx[slot, rows, span(c)].astype(jnp.float32) * scale
            out_ref[rows, span(c)] = total

    own_half, other_half = range(slices), range(slices, 2 * slices)
    build(2, own_half)
    code_relay().wait_recv()
    build(2, other_half)
    build(1, range(2 * slices))
    build(0, range(2 * slices))
    start_relay(0)
    if last >= 2:
        start_xy(2)
    partial(0, 2, pl.ds(0, half))
    partial(0, 1, pl.ds(0, half))
    waiting = []
    for c in range(last + 1):
        waiting.append(c)
        for copy in relay_copies(c):
            copy.wait_recv()
        rest = dict(tokens=pl.ds(half, half), base=True) if c == 0 else {}
        top = partial(c, 2, **rest)
        pl.when(edge)(lambda: send(c, 2, top, 1, near_z))
        top = partial(c, 1, **rest)
        pl.when(edge)(lambda: send(c, 1, top, 2, near_z))
        if c == 0 and last >= 1:
            start_relay(1)
        send(c, 0, partial(c, 0), 0, near_z)
        if c and c + 1 <= last:
            start_relay(c + 1)
        if c + 3 <= last:
            start_xy(c + 3)
        if c == min(2, last):
            build(3, range(2 * slices))
        for late in [w for w in waiting if c >= 2 and w < max(c, 2) or c == last]:
            partial(late, 3)
            waiting.remove(late)

        @pl.when(inner)
        def _():
            if c >= 1:
                combine(c - 1, 2, 1, 1, far_z)
                combine(c - 1, 1, 2, 3, mid_z)
            if c >= 2:
                add(c - 2, (0, 3))

        if c >= 3:
            pl.when(edge)(lambda: add(c - 3, (0, 1)))

    @pl.when(inner)
    def _():
        combine(last, 2, 1, 1, far_z)
        combine(last, 1, 2, 3, mid_z)
        for c in range(max(last - 1, 0), last + 1):
            add(c, (0, 3))

    @pl.when(edge)
    def _():
        for c in range(max(last - 2, 0), last + 1):
            add(c, (0, 1))

    code_relay().wait_send()
    for s in range(1, slices):
        code_copy(s).wait_send()
    for c in range(last + 1):
        for s in range(1, slices):
            xy_copy(c, s).wait_send()
        for copy in relay_copies(c):
            copy.wait_send()
        for i in range(3):
            for copy in line_copies(c, i, 0, near_z):
                copy.wait_send()


def local_line(cotangent, token_owner, token_row, params, moment_one, moment_two):
    slices = lax.axis_size("dp")
    toks = cotangent.shape[0]
    own_rows, cols = params.shape
    tiles = cols // LANES
    marks = sorted({tiles * share // SHARES[-1] for share in SHARES})
    chunks = [(a * LANES, (b - a) * LANES) for a, b in zip(marks[:-1], marks[1:])]
    count = len(chunks)
    dma = pltpu.SemaphoreType.DMA
    operands = (token_owner.reshape(1, toks), token_row.reshape(1, toks), cotangent)
    grads = pl.pallas_call(
        functools.partial(line_kernel, slices, chunks),
        out_shape=jax.ShapeDtypeStruct((own_rows, cols), jnp.float32),
        in_specs=[pl.BlockSpec(memory_space=pltpu.HBM)] * 3,
        out_specs=pl.BlockSpec(memory_space=pltpu.VMEM),
        scratch_shapes=[
            pltpu.VMEM((2 * slices * toks, cols), jnp.bfloat16),
            pltpu.VMEM((1, toks), jnp.int32),
            pltpu.VMEM((1, toks), jnp.int32),
            pltpu.VMEM((2 * slices, 1, toks), jnp.int32),
            pltpu.VMEM((4, own_rows, 2 * slices * toks), jnp.bfloat16),
            pltpu.VMEM((2, 3, own_rows, max(size for _, size in chunks)), jnp.float32),
            pltpu.VMEM((3, own_rows, cols), jnp.int16),
            pltpu.VMEM((3, 1, cols), jnp.float32),
            pltpu.VMEM((4, own_rows, cols), jnp.int16),
            pltpu.VMEM((4, 1, cols), jnp.float32),
            dma((3,)), dma((slices,)), dma((slices,)),
            dma((count, slices)), dma((count, slices)), dma((count, slices)), dma((count, slices)),
            dma((count, 3)), dma((count, 4)), dma((count, 3)), dma((count, 4)),
        ],
        name="line_sums",
        compiler_params=pltpu.CompilerParams(
            collective_id=0, has_side_effects=True, vmem_limit_bytes=VMEM_MIB * 1024 * 1024
        ),
    )(*(pltpu.with_memory_space_constraint(a, pltpu.HBM) for a in operands))
    return adam(grads, params, moment_one, moment_two)


def solution(mesh):
    placed = (
        P(("dp", "vocab"), None),
        P(("dp", "vocab"), None),
        P(("dp", "vocab")),
        P("vocab", "dp"),
        P("vocab", "dp"),
        P("vocab", "dp"),
    )
    slices = mesh.shape["dp"]
    line = mesh.shape["vocab"] == 2 * 4 and slices & (slices - 1) == 0
    return jax.shard_map(
        local_line if line else local_general,
        mesh=mesh,
        in_specs=placed,
        out_specs=(P("vocab", "dp"), P("vocab", "dp"), P("vocab", "dp")),
        check_vma=False,
    )
```

```python
import functools

import jax
import jax.numpy as jnp
from jax import lax
from jax.experimental import pallas as pl
from jax.experimental.pallas import tpu as pltpu
from jax.sharding import PartitionSpec as P

beta_first = 0.9
beta_second = 0.999
learning = 0.01
epsilon = 1e-08
correct_second = 0.6323045752290363

LANES = 128
TILE = 128
DOT_TILE = 256
LEVELS = 32767.0
VMEM_MIB = 46
SHARES = (0, 1, 2, 3, 5, 7, 9)
MESH = pl.DeviceIdType.MESH


def bucket(cotangent, owner_list, token_row, owners, capacity):
    owner_hot = (owner_list[:, None] == jnp.arange(owners, dtype=jnp.int32)[None, :]).astype(
        jnp.int32
    )
    order = jnp.arange(owner_list.shape[0], dtype=jnp.int32)
    before = (order[None, :] < order[:, None]).astype(jnp.bfloat16)
    earlier = jnp.dot(
        before, owner_hot.astype(jnp.bfloat16), preferred_element_type=jnp.float32
    ).astype(jnp.int32)
    slot_index = jnp.sum(earlier * owner_hot, axis=1)
    target = owner_list * capacity + slot_index
    places = jnp.arange(owners * capacity, dtype=jnp.int32)
    matches = places[:, None] == target[None, :]
    outgoing = jnp.dot(matches.astype(jnp.bfloat16), cotangent, preferred_element_type=jnp.float32)
    outgoing = outgoing.astype(jnp.bfloat16).reshape(owners, capacity, cotangent.shape[1])
    row_index = jnp.max(jnp.where(matches, token_row[None, :], -1), axis=1).reshape(
        owners, capacity
    )
    return (outgoing, row_index)


def adam(grads, params, moment_one, moment_two):
    new_first = beta_first * moment_one + (1.0 - beta_first) * grads
    new_second = beta_second * moment_two + (1.0 - beta_second) * grads * grads
    step_size = new_first / (jnp.sqrt(new_second / correct_second) + epsilon)
    new_params = params - learning * step_size
    return (new_params, new_first, new_second)


def local_general(cotangent, token_owner, token_row, params, moment_one, moment_two):
    owners = lax.axis_size("vocab")
    tok_count, width = cotangent.shape
    capacity = 2 * tok_count // owners
    own_rows = params.shape[0]
    outgoing, row_index = bucket(cotangent, token_owner[:, 0], token_row, owners, capacity)
    arrived, arrived_rows = (
        lax.all_to_all(outgoing, "vocab", split_axis=0, concat_axis=0, tiled=True),
        lax.all_to_all(row_index, "vocab", split_axis=0, concat_axis=0, tiled=True),
    )
    selector = (
        jnp.arange(own_rows, dtype=jnp.int32)[:, None] == arrived_rows.reshape(-1)[None, :]
    ).astype(jnp.bfloat16)
    full_grads = jnp.dot(
        selector, arrived.reshape(owners * capacity, width), preferred_element_type=jnp.float32
    )
    grads = lax.psum_scatter(full_grads, "dp", scatter_dimension=1, tiled=True)
    return adam(grads, params, moment_one, moment_two)


def flipped(index, bits):
    bit = 1
    while bit <= bits:
        if bits & bit:
            index = index + bit * (1 - 2 * lax.rem(lax.div(index, bit), 2))
        bit *= 2
    return index


def line_kernel(
    slices, chunks, owner_ref, row_ref, cot_ref, out_ref,
    held, owner_own, row_own, code_of, sel, acc, tx, txs, rx, rxs,
    own_sem, code_send, code_recv, xy_send, xy_recv, relay_send, relay_recv, z_send, z_recv, s_send, s_recv,
):
    d = lax.axis_index("dp")
    v = lax.axis_index("vocab")
    z, core = lax.div(v, 2), lax.rem(v, 2)
    partner = flipped(v, 1)
    toks = cot_ref.shape[0]
    own_rows, cols = out_ref.shape
    half = slices * toks
    last = len(chunks) - 1
    edge = (z == 0) | (z == 3)
    inner = (z == 1) | (z == 2)
    low = lax.div(z, 2)
    mid_z, far_z = 2 - low, 3 - 3 * low
    near_z = flipped(z, 1)
    places = (near_z, mid_z, far_z, z)

    def at(dp, vocab):
        return {"dp": dp, "vocab": vocab}

    def remote(src, dst, send, recv, peer):
        return pltpu.make_async_remote_copy(
            src_ref=src, dst_ref=dst, send_sem=send, recv_sem=recv, device_id=peer,
            device_id_type=MESH,
        )

    def span(c):
        start, size = chunks[c]
        return pl.ds(start, size)

    def code_copy(s):
        return remote(
            code_of.at[0], code_of.at[s], code_send.at[s], code_recv.at[s], at(flipped(d, s), v)
        )

    def code_relay():
        return remote(
            code_of.at[pl.ds(0, slices)], code_of.at[pl.ds(slices, slices)],
            code_send.at[0], code_recv.at[0], at(d, partner),
        )

    def xy_copy(c, s):
        start, size = chunks[c]
        peer = flipped(d, s)
        first = pl.multiple_of(peer * cols + start, LANES)
        return remote(
            cot_ref.at[:, pl.ds(first, size)], held.at[pl.ds(s * toks, toks), span(c)],
            xy_send.at[c, s], xy_recv.at[c, s], at(peer, v),
        )

    def relay_copies(c):
        pieces = [(s * toks, toks) for s in [*reversed(range(1, slices)), 0]] if c == 0 else [(0, half)]
        return [
            remote(
                held.at[pl.ds(row, size), span(c)], held.at[pl.ds(half + row, size), span(c)],
                relay_send.at[c, n], relay_recv.at[c, n], at(d, partner),
            )
            for n, (row, size) in enumerate(pieces)
        ]

    def line_copies(c, i, slot, to):
        peer = at(d, to * 2 + core)
        return (
            remote(
                txs.at[i, :, span(c)], rxs.at[slot, :, span(c)],
                s_send.at[c, i], s_recv.at[c, slot], peer,
            ),
            remote(
                tx.at[i, :, span(c)], rx.at[slot, :, span(c)],
                z_send.at[c, i], z_recv.at[c, slot], peer,
            ),
        )

    def start_xy(c):
        for s in reversed(range(1, slices)):
            xy_copy(c, s).start()

    def start_relay(c):
        copies = relay_copies(c)
        if c == 0:
            copies.pop().start()
        for s in reversed(range(1, slices)):
            xy_copy(c, s).wait_recv()
            if c == 0:
                copies.pop(0).start()
        if c:
            copies[0].start()

    first = pl.multiple_of(d * cols, LANES)
    own_copies = [
        pltpu.make_async_copy(owner_ref, owner_own, own_sem.at[0]),
        pltpu.make_async_copy(row_ref, row_own, own_sem.at[1]),
        pltpu.make_async_copy(
            cot_ref.at[:, pl.ds(first, cols)], held.at[pl.ds(0, toks), :], own_sem.at[2]
        ),
    ]
    for copy in own_copies:
        copy.start()

    barrier = pltpu.get_barrier_semaphore()
    greeted = [at(flipped(d, s), v) for s in range(1, slices)] + [at(d, partner)]
    greeted += [at(d, lax.rem(v + 2 * s, 8)) for s in range(1, 4)]
    for peer in greeted:
        pl.semaphore_signal(barrier, inc=1, device_id=peer, device_id_type=MESH)
    own_copies[0].wait()
    own_copies[1].wait()
    code_of[0] = owner_own[...] * own_rows + row_own[...]
    pl.semaphore_wait(barrier, len(greeted))

    for s in reversed(range(1, slices)):
        code_copy(s).start()
    start_xy(0)
    if last >= 1:
        start_xy(1)
    for s in range(1, slices):
        code_copy(s).wait_recv()
    code_relay().start()
    own_copies[2].wait()

    def build(i, parts):
        base = (places[i] * 2 + core) * own_rows
        for b in parts:
            code = code_of[b] - base

            @pl.loop(0, own_rows // TILE)
            def _(r):
                first = pl.multiple_of(r * TILE, TILE)
                rows = lax.broadcasted_iota(jnp.int32, (TILE, toks), 0)
                sel[i, pl.ds(first, TILE), pl.ds(b * toks, toks)] = jnp.where(
                    rows == code - first, 1.0, 0.0
                ).astype(jnp.bfloat16)

    def partial(c, i, tokens=None, base=False):
        start, size = chunks[c]
        tokens = pl.ds(0, 2 * half) if tokens is None else tokens

        def body(r, top):
            rows = pl.ds(pl.multiple_of(r * DOT_TILE, DOT_TILE), DOT_TILE)
            part = jnp.dot(
                sel[i, rows, tokens], held[tokens, span(c)], preferred_element_type=jnp.float32
            )
            if base:
                part = part + acc[c % 2, i, rows, pl.ds(0, size)]
            if i == 3:
                out_ref[rows, span(c)] = part
            else:
                acc[c % 2, i, rows, pl.ds(0, size)] = part
            return jnp.maximum(top, jnp.max(jnp.abs(part), axis=0, keepdims=True))

        return lax.fori_loop(0, own_rows // DOT_TILE, body, jnp.zeros((1, size), jnp.float32))

    def send(c, i, top, slot, to):
        start, size = chunks[c]
        bound = jnp.maximum(top, 1e-30)
        txs[i, :, span(c)] = bound * (1.0 / LEVELS)
        factor = LEVELS / bound

        @pl.loop(0, own_rows // TILE)
        def _(r):
            rows = pl.ds(pl.multiple_of(r * TILE, TILE), TILE)
            scaled = jnp.round(acc[c % 2, i, rows, pl.ds(0, size)] * factor)
            tx[i, rows, span(c)] = scaled.astype(jnp.int32).astype(jnp.int16)

        for copy in line_copies(c, i, slot, to):
            copy.start()

    def arrived(c, slot):
        for copy in line_copies(c, 0, slot, near_z):
            copy.wait_recv()
        return rxs[slot, :, span(c)]

    def combine(c, i, rx_slot, slot, to):
        start, size = chunks[c]
        scale = arrived(c, rx_slot)

        def body(r, top):
            rows = pl.ds(pl.multiple_of(r * TILE, TILE), TILE)
            wide = pl.ds(0, size)
            both = acc[c % 2, i, rows, wide] + rx[rx_slot, rows, span(c)].astype(jnp.float32) * scale
            acc[c % 2, i, rows, wide] = both
            return jnp.maximum(top, jnp.max(jnp.abs(both), axis=0, keepdims=True))

        top = lax.fori_loop(0, own_rows // TILE, body, jnp.zeros((1, size), jnp.float32))
        send(c, i, top, slot, to)

    def add(c, slots):
        scales = [arrived(c, slot) for slot in slots]

        @pl.loop(0, own_rows // TILE)
        def _(r):
            rows = pl.ds(pl.multiple_of(r * TILE, TILE), TILE)
            total = out_ref[rows, span(c)]
            for slot, scale in zip(slots, scales):
                total = total + rx[slot, rows, span(c)].astype(jnp.float32) * scale
            out_ref[rows, span(c)] = total

    own_half, other_half = range(slices), range(slices, 2 * slices)
    build(2, own_half)
    code_relay().wait_recv()
    build(2, other_half)
    build(1, range(2 * slices))
    build(0, range(2 * slices))
    start_relay(0)
    for c in range(2, last + 1):
        start_xy(c)
    partial(0, 2, pl.ds(0, half))
    partial(0, 1, pl.ds(0, half))
    waiting = []
    for c in range(last + 1):
        waiting.append(c)
        for copy in relay_copies(c):
            copy.wait_recv()
        rest = dict(tokens=pl.ds(half, half), base=True) if c == 0 else {}
        top = partial(c, 2, **rest)
        pl.when(edge)(lambda: send(c, 2, top, 1, near_z))
        top = partial(c, 1, **rest)
        pl.when(edge)(lambda: send(c, 1, top, 2, near_z))
        if c == 0 and last >= 1:
            start_relay(1)
        send(c, 0, partial(c, 0), 0, near_z)
        if c and c + 1 <= last:
            start_relay(c + 1)
        if c == min(2, last):
            build(3, range(2 * slices))
        for late in [w for w in waiting if c >= 2 and w < max(c, 2) or c == last]:
            partial(late, 3)
            waiting.remove(late)

        @pl.when(inner)
        def _():
            if c >= 1:
                combine(c - 1, 2, 1, 1, far_z)
                combine(c - 1, 1, 2, 3, mid_z)
            if c >= 2:
                add(c - 2, (0, 3))

        if c >= 3:
            pl.when(edge)(lambda: add(c - 3, (0, 1)))

    @pl.when(inner)
    def _():
        combine(last, 2, 1, 1, far_z)
        combine(last, 1, 2, 3, mid_z)
        for c in range(max(last - 1, 0), last + 1):
            add(c, (0, 3))

    @pl.when(edge)
    def _():
        for c in range(max(last - 2, 0), last + 1):
            add(c, (0, 1))

    code_relay().wait_send()
    for s in range(1, slices):
        code_copy(s).wait_send()
    for c in range(last + 1):
        for s in range(1, slices):
            xy_copy(c, s).wait_send()
        for copy in relay_copies(c):
            copy.wait_send()
        for i in range(3):
            for copy in line_copies(c, i, 0, near_z):
                copy.wait_send()


def local_line(cotangent, token_owner, token_row, params, moment_one, moment_two):
    slices = lax.axis_size("dp")
    toks = cotangent.shape[0]
    own_rows, cols = params.shape
    tiles = cols // LANES
    marks = sorted({tiles * share // SHARES[-1] for share in SHARES})
    chunks = [(a * LANES, (b - a) * LANES) for a, b in zip(marks[:-1], marks[1:])]
    count = len(chunks)
    dma = pltpu.SemaphoreType.DMA
    operands = (token_owner.reshape(1, toks), token_row.reshape(1, toks), cotangent)
    grads = pl.pallas_call(
        functools.partial(line_kernel, slices, chunks),
        out_shape=jax.ShapeDtypeStruct((own_rows, cols), jnp.float32),
        in_specs=[pl.BlockSpec(memory_space=pltpu.HBM)] * 3,
        out_specs=pl.BlockSpec(memory_space=pltpu.VMEM),
        scratch_shapes=[
            pltpu.VMEM((2 * slices * toks, cols), jnp.bfloat16),
            pltpu.VMEM((1, toks), jnp.int32),
            pltpu.VMEM((1, toks), jnp.int32),
            pltpu.VMEM((2 * slices, 1, toks), jnp.int32),
            pltpu.VMEM((4, own_rows, 2 * slices * toks), jnp.bfloat16),
            pltpu.VMEM((2, 3, own_rows, max(size for _, size in chunks)), jnp.float32),
            pltpu.VMEM((3, own_rows, cols), jnp.int16),
            pltpu.VMEM((3, 1, cols), jnp.float32),
            pltpu.VMEM((4, own_rows, cols), jnp.int16),
            pltpu.VMEM((4, 1, cols), jnp.float32),
            dma((3,)), dma((slices,)), dma((slices,)),
            dma((count, slices)), dma((count, slices)), dma((count, slices)), dma((count, slices)),
            dma((count, 3)), dma((count, 4)), dma((count, 3)), dma((count, 4)),
        ],
        name="line_sums",
        compiler_params=pltpu.CompilerParams(
            collective_id=0, has_side_effects=True, vmem_limit_bytes=VMEM_MIB * 1024 * 1024
        ),
    )(*(pltpu.with_memory_space_constraint(a, pltpu.HBM) for a in operands))
    return adam(grads, params, moment_one, moment_two)


def solution(mesh):
    placed = (
        P(("dp", "vocab"), None),
        P(("dp", "vocab"), None),
        P(("dp", "vocab")),
        P("vocab", "dp"),
        P("vocab", "dp"),
        P("vocab", "dp"),
    )
    slices = mesh.shape["dp"]
    line = mesh.shape["vocab"] == 2 * 4 and slices & (slices - 1) == 0
    return jax.shard_map(
        local_line if line else local_general,
        mesh=mesh,
        in_specs=placed,
        out_specs=(P("vocab", "dp"), P("vocab", "dp"), P("vocab", "dp")),
        check_vma=False,
    )
```

```python
import functools

import jax
import jax.numpy as jnp
from jax import lax
from jax.experimental import pallas as pl
from jax.experimental.pallas import tpu as pltpu
from jax.sharding import PartitionSpec as P

beta_first = 0.9
beta_second = 0.999
learning = 0.01
epsilon = 1e-08
correct_second = 0.6323045752290363

LANES = 128
TILE = 128
DOT_TILE = 256
LEVELS = 32767.0
VMEM_MIB = 46
SHARES = (0, 1, 2, 3, 5, 7, 9)
MESH = pl.DeviceIdType.MESH


def bucket(cotangent, owner_list, token_row, owners, capacity):
    owner_hot = (owner_list[:, None] == jnp.arange(owners, dtype=jnp.int32)[None, :]).astype(
        jnp.int32
    )
    order = jnp.arange(owner_list.shape[0], dtype=jnp.int32)
    before = (order[None, :] < order[:, None]).astype(jnp.bfloat16)
    earlier = jnp.dot(
        before, owner_hot.astype(jnp.bfloat16), preferred_element_type=jnp.float32
    ).astype(jnp.int32)
    slot_index = jnp.sum(earlier * owner_hot, axis=1)
    target = owner_list * capacity + slot_index
    places = jnp.arange(owners * capacity, dtype=jnp.int32)
    matches = places[:, None] == target[None, :]
    outgoing = jnp.dot(matches.astype(jnp.bfloat16), cotangent, preferred_element_type=jnp.float32)
    outgoing = outgoing.astype(jnp.bfloat16).reshape(owners, capacity, cotangent.shape[1])
    row_index = jnp.max(jnp.where(matches, token_row[None, :], -1), axis=1).reshape(
        owners, capacity
    )
    return (outgoing, row_index)


def adam(grads, params, moment_one, moment_two):
    new_first = beta_first * moment_one + (1.0 - beta_first) * grads
    new_second = beta_second * moment_two + (1.0 - beta_second) * grads * grads
    step_size = new_first / (jnp.sqrt(new_second / correct_second) + epsilon)
    new_params = params - learning * step_size
    return (new_params, new_first, new_second)


def local_general(cotangent, token_owner, token_row, params, moment_one, moment_two):
    owners = lax.axis_size("vocab")
    tok_count, width = cotangent.shape
    capacity = 2 * tok_count // owners
    own_rows = params.shape[0]
    outgoing, row_index = bucket(cotangent, token_owner[:, 0], token_row, owners, capacity)
    arrived, arrived_rows = (
        lax.all_to_all(outgoing, "vocab", split_axis=0, concat_axis=0, tiled=True),
        lax.all_to_all(row_index, "vocab", split_axis=0, concat_axis=0, tiled=True),
    )
    selector = (
        jnp.arange(own_rows, dtype=jnp.int32)[:, None] == arrived_rows.reshape(-1)[None, :]
    ).astype(jnp.bfloat16)
    full_grads = jnp.dot(
        selector, arrived.reshape(owners * capacity, width), preferred_element_type=jnp.float32
    )
    grads = lax.psum_scatter(full_grads, "dp", scatter_dimension=1, tiled=True)
    return adam(grads, params, moment_one, moment_two)


def flipped(index, bits):
    bit = 1
    while bit <= bits:
        if bits & bit:
            index = index + bit * (1 - 2 * lax.rem(lax.div(index, bit), 2))
        bit *= 2
    return index


def line_kernel(
    slices, chunks, owner_ref, row_ref, cot_ref, out_ref,
    held, owner_own, row_own, code_of, sel, acc, tx, txs, rx, rxs,
    own_sem, code_send, code_recv, xy_send, xy_recv, relay_send, relay_recv, z_send, z_recv, s_send, s_recv,
):
    d = lax.axis_index("dp")
    v = lax.axis_index("vocab")
    z, core = lax.div(v, 2), lax.rem(v, 2)
    partner = flipped(v, 1)
    toks = cot_ref.shape[0]
    own_rows, cols = out_ref.shape
    half = slices * toks
    last = len(chunks) - 1
    edge = (z == 0) | (z == 3)
    inner = (z == 1) | (z == 2)
    low = lax.div(z, 2)
    mid_z, far_z = 2 - low, 3 - 3 * low
    near_z = flipped(z, 1)
    places = (near_z, mid_z, far_z, z)

    def at(dp, vocab):
        return {"dp": dp, "vocab": vocab}

    def remote(src, dst, send, recv, peer):
        return pltpu.make_async_remote_copy(
            src_ref=src, dst_ref=dst, send_sem=send, recv_sem=recv, device_id=peer,
            device_id_type=MESH,
        )

    def span(c):
        start, size = chunks[c]
        return pl.ds(start, size)

    def code_copy(s):
        return remote(
            code_of.at[0], code_of.at[s], code_send.at[s], code_recv.at[s], at(flipped(d, s), v)
        )

    def code_relay():
        return remote(
            code_of.at[pl.ds(0, slices)], code_of.at[pl.ds(slices, slices)],
            code_send.at[0], code_recv.at[0], at(d, partner),
        )

    def xy_copy(c, s):
        start, size = chunks[c]
        peer = flipped(d, s)
        first = pl.multiple_of(peer * cols + start, LANES)
        return remote(
            cot_ref.at[:, pl.ds(first, size)], held.at[pl.ds(s * toks, toks), span(c)],
            xy_send.at[c, s], xy_recv.at[c, s], at(peer, v),
        )

    def relay_copies(c):
        pieces = [(s * toks, toks) for s in [*reversed(range(1, slices)), 0]] if c == 0 else [(0, half)]
        return [
            remote(
                held.at[pl.ds(row, size), span(c)], held.at[pl.ds(half + row, size), span(c)],
                relay_send.at[c, n], relay_recv.at[c, n], at(d, partner),
            )
            for n, (row, size) in enumerate(pieces)
        ]

    def line_copies(c, i, slot, to):
        peer = at(d, to * 2 + core)
        return (
            remote(
                txs.at[i, :, span(c)], rxs.at[slot, :, span(c)],
                s_send.at[c, i], s_recv.at[c, slot], peer,
            ),
            remote(
                tx.at[i, :, span(c)], rx.at[slot, :, span(c)],
                z_send.at[c, i], z_recv.at[c, slot], peer,
            ),
        )

    def start_xy(c):
        for s in reversed(range(1, slices)):
            xy_copy(c, s).start()

    def start_relay(c):
        copies = relay_copies(c)
        if c == 0:
            copies.pop().start()
        for s in reversed(range(1, slices)):
            xy_copy(c, s).wait_recv()
            if c == 0:
                copies.pop(0).start()
        if c:
            copies[0].start()

    first = pl.multiple_of(d * cols, LANES)
    own_copies = [
        pltpu.make_async_copy(owner_ref, owner_own, own_sem.at[0]),
        pltpu.make_async_copy(row_ref, row_own, own_sem.at[1]),
        pltpu.make_async_copy(
            cot_ref.at[:, pl.ds(first, cols)], held.at[pl.ds(0, toks), :], own_sem.at[2]
        ),
    ]
    for copy in own_copies:
        copy.start()

    barrier = pltpu.get_barrier_semaphore()
    greeted = [at(flipped(d, s), v) for s in range(1, slices)] + [at(d, partner)]
    greeted += [at(d, lax.rem(v + 2 * s, 8)) for s in range(1, 4)]
    for peer in greeted:
        pl.semaphore_signal(barrier, inc=1, device_id=peer, device_id_type=MESH)
    own_copies[0].wait()
    own_copies[1].wait()
    code_of[0] = owner_own[...] * own_rows + row_own[...]
    pl.semaphore_wait(barrier, len(greeted))

    for s in reversed(range(1, slices)):
        code_copy(s).start()
    start_xy(0)
    if last >= 1:
        start_xy(1)
    for s in range(1, slices):
        code_copy(s).wait_recv()
    code_relay().start()
    own_copies[2].wait()

    def build(i, parts):
        base = (places[i] * 2 + core) * own_rows
        for b in parts:
            code = code_of[b] - base

            @pl.loop(0, own_rows // TILE)
            def _(r):
                first = pl.multiple_of(r * TILE, TILE)
                rows = lax.broadcasted_iota(jnp.int32, (TILE, toks), 0)
                sel[i, pl.ds(first, TILE), pl.ds(b * toks, toks)] = jnp.where(
                    rows == code - first, 1.0, 0.0
                ).astype(jnp.bfloat16)

    def partial(c, i, tokens=None, base=False):
        start, size = chunks[c]
        tokens = pl.ds(0, 2 * half) if tokens is None else tokens

        def body(r, top):
            rows = pl.ds(pl.multiple_of(r * DOT_TILE, DOT_TILE), DOT_TILE)
            part = jnp.dot(
                sel[i, rows, tokens], held[tokens, span(c)], preferred_element_type=jnp.float32
            )
            if base:
                part = part + acc[c % 2, i, rows, pl.ds(0, size)]
            if i == 3:
                out_ref[rows, span(c)] = part
            else:
                acc[c % 2, i, rows, pl.ds(0, size)] = part
            return jnp.maximum(top, jnp.max(jnp.abs(part), axis=0, keepdims=True))

        return lax.fori_loop(0, own_rows // DOT_TILE, body, jnp.zeros((1, size), jnp.float32))

    def send(c, i, top, slot, to):
        start, size = chunks[c]
        bound = jnp.maximum(top, 1e-30)
        txs[i, :, span(c)] = bound * (1.0 / LEVELS)
        factor = LEVELS / bound

        @pl.loop(0, own_rows // TILE)
        def _(r):
            rows = pl.ds(pl.multiple_of(r * TILE, TILE), TILE)
            scaled = jnp.round(acc[c % 2, i, rows, pl.ds(0, size)] * factor)
            tx[i, rows, span(c)] = scaled.astype(jnp.int32).astype(jnp.int16)

        for copy in line_copies(c, i, slot, to):
            copy.start()

    def arrived(c, slot):
        for copy in line_copies(c, 0, slot, near_z):
            copy.wait_recv()
        return rxs[slot, :, span(c)]

    def combine(c, i, rx_slot, slot, to):
        start, size = chunks[c]
        scale = arrived(c, rx_slot)

        def body(r, top):
            rows = pl.ds(pl.multiple_of(r * TILE, TILE), TILE)
            wide = pl.ds(0, size)
            both = acc[c % 2, i, rows, wide] + rx[rx_slot, rows, span(c)].astype(jnp.float32) * scale
            acc[c % 2, i, rows, wide] = both
            return jnp.maximum(top, jnp.max(jnp.abs(both), axis=0, keepdims=True))

        top = lax.fori_loop(0, own_rows // TILE, body, jnp.zeros((1, size), jnp.float32))
        send(c, i, top, slot, to)

    def add(c, slots):
        scales = [arrived(c, slot) for slot in slots]

        @pl.loop(0, own_rows // TILE)
        def _(r):
            rows = pl.ds(pl.multiple_of(r * TILE, TILE), TILE)
            total = out_ref[rows, span(c)]
            for slot, scale in zip(slots, scales):
                total = total + rx[slot, rows, span(c)].astype(jnp.float32) * scale
            out_ref[rows, span(c)] = total

    own_half, other_half = range(slices), range(slices, 2 * slices)
    build(2, own_half)
    code_relay().wait_recv()
    build(2, other_half)
    build(1, range(2 * slices))
    build(0, range(2 * slices))
    start_relay(0)
    if last >= 2:
        start_xy(2)
    partial(0, 2, pl.ds(0, half))
    partial(0, 1, pl.ds(0, half))
    waiting = []
    for c in range(last + 1):
        waiting.append(c)
        for copy in relay_copies(c):
            copy.wait_recv()
        rest = dict(tokens=pl.ds(half, half), base=True) if c == 0 else {}
        top = partial(c, 2, **rest)
        pl.when(edge)(lambda: send(c, 2, top, 1, near_z))
        top = partial(c, 1, **rest)
        pl.when(edge)(lambda: send(c, 1, top, 2, near_z))
        if c == 0 and last >= 1:
            for ahead in range(3, last + 1):
                start_xy(ahead)
            start_relay(1)
        send(c, 0, partial(c, 0), 0, near_z)
        if c and c + 1 <= last:
            start_relay(c + 1)
        if c == min(2, last):
            build(3, range(2 * slices))
        for late in [w for w in waiting if c >= 2 and w < max(c, 2) or c == last]:
            partial(late, 3)
            waiting.remove(late)

        @pl.when(inner)
        def _():
            if c >= 1:
                combine(c - 1, 2, 1, 1, far_z)
                combine(c - 1, 1, 2, 3, mid_z)
            if c >= 2:
                add(c - 2, (0, 3))

        if c >= 3:
            pl.when(edge)(lambda: add(c - 3, (0, 1)))

    @pl.when(inner)
    def _():
        combine(last, 2, 1, 1, far_z)
        combine(last, 1, 2, 3, mid_z)
        for c in range(max(last - 1, 0), last + 1):
            add(c, (0, 3))

    @pl.when(edge)
    def _():
        for c in range(max(last - 2, 0), last + 1):
            add(c, (0, 1))

    code_relay().wait_send()
    for s in range(1, slices):
        code_copy(s).wait_send()
    for c in range(last + 1):
        for s in range(1, slices):
            xy_copy(c, s).wait_send()
        for copy in relay_copies(c):
            copy.wait_send()
        for i in range(3):
            for copy in line_copies(c, i, 0, near_z):
                copy.wait_send()


def local_line(cotangent, token_owner, token_row, params, moment_one, moment_two):
    slices = lax.axis_size("dp")
    toks = cotangent.shape[0]
    own_rows, cols = params.shape
    tiles = cols // LANES
    marks = sorted({tiles * share // SHARES[-1] for share in SHARES})
    chunks = [(a * LANES, (b - a) * LANES) for a, b in zip(marks[:-1], marks[1:])]
    count = len(chunks)
    dma = pltpu.SemaphoreType.DMA
    operands = (token_owner.reshape(1, toks), token_row.reshape(1, toks), cotangent)
    grads = pl.pallas_call(
        functools.partial(line_kernel, slices, chunks),
        out_shape=jax.ShapeDtypeStruct((own_rows, cols), jnp.float32),
        in_specs=[pl.BlockSpec(memory_space=pltpu.HBM)] * 3,
        out_specs=pl.BlockSpec(memory_space=pltpu.VMEM),
        scratch_shapes=[
            pltpu.VMEM((2 * slices * toks, cols), jnp.bfloat16),
            pltpu.VMEM((1, toks), jnp.int32),
            pltpu.VMEM((1, toks), jnp.int32),
            pltpu.VMEM((2 * slices, 1, toks), jnp.int32),
            pltpu.VMEM((4, own_rows, 2 * slices * toks), jnp.bfloat16),
            pltpu.VMEM((2, 3, own_rows, max(size for _, size in chunks)), jnp.float32),
            pltpu.VMEM((3, own_rows, cols), jnp.int16),
            pltpu.VMEM((3, 1, cols), jnp.float32),
            pltpu.VMEM((4, own_rows, cols), jnp.int16),
            pltpu.VMEM((4, 1, cols), jnp.float32),
            dma((3,)), dma((slices,)), dma((slices,)),
            dma((count, slices)), dma((count, slices)), dma((count, slices)), dma((count, slices)),
            dma((count, 3)), dma((count, 4)), dma((count, 3)), dma((count, 4)),
        ],
        name="line_sums",
        compiler_params=pltpu.CompilerParams(
            collective_id=0, has_side_effects=True, vmem_limit_bytes=VMEM_MIB * 1024 * 1024
        ),
    )(*(pltpu.with_memory_space_constraint(a, pltpu.HBM) for a in operands))
    return adam(grads, params, moment_one, moment_two)


def solution(mesh):
    placed = (
        P(("dp", "vocab"), None),
        P(("dp", "vocab"), None),
        P(("dp", "vocab")),
        P("vocab", "dp"),
        P("vocab", "dp"),
        P("vocab", "dp"),
    )
    slices = mesh.shape["dp"]
    line = mesh.shape["vocab"] == 2 * 4 and slices & (slices - 1) == 0
    return jax.shard_map(
        local_line if line else local_general,
        mesh=mesh,
        in_specs=placed,
        out_specs=(P("vocab", "dp"), P("vocab", "dp"), P("vocab", "dp")),
        check_vma=False,
    )
```
